32 devices in a mesh: fsdp: 4 (over x, core), ctx: 4 (over z), tp: 2 (over y).
Axes of the slice: x: 2, y: 2, z: 4, core: 2. Of those that a mesh axis runs over, the one named last changes fastest.
Arguments:
- block_input: bfloat16 [4, 1024, 2048], P('fsdp', 'ctx'), may hold values from -6 to 6
- lengths: int32 [4, 6], P('fsdp'), may hold values from 1 to 512, 1024 in all within a row
- norm_scales: bfloat16 [2, 2048], P(None, 'fsdp'), may hold values from 0.099609375 to 1.8984375
- norm_biases: bfloat16 [2, 2048], P(None, 'fsdp'), may hold values from -3 to 3
- qkv_weight: bfloat16 [3, 2048, 2048], P(None, 'fsdp', 'tp'), may hold values from -0.125 to 0.125
- qkv_bias: bfloat16 [3, 32, 64], P(None, 'tp', 'fsdp'), may hold values from -7.3 to 7.3
- out_weight: bfloat16 [2048, 2048], P('tp', 'fsdp'), may hold values from -2 to 2
- gate_up_weight: bfloat16 [2, 2048, 5632], P(None, 'fsdp', 'tp'), may hold values from -0.125 to 0.125
- down_weight: bfloat16 [5632, 2048], P('tp', 'fsdp'), may hold values from -0.109375 to 0.109375
- out_cotangent: bfloat16 [4, 1024, 2048], P('fsdp', 'ctx'), may hold values from -6 to 6
Outputs:
- block_output: bfloat16 [4, 1024, 2048], P('fsdp', 'ctx')
- input_grad: float32 [4, 1024, 2048], P('fsdp', 'ctx')
- norm_scales_grad: float32 [2, 2048], P(None, 'fsdp')
- norm_biases_grad: float32 [2, 2048], P(None, 'fsdp')
- qkv_weight_grad: float32 [3, 2048, 2048], P(None, 'fsdp', 'tp')
- qkv_bias_grad: float32 [3, 32, 64], P(None, 'tp', 'fsdp')
- out_weight_grad: float32 [2048, 2048], P('tp', 'fsdp')
- gate_up_weight_grad: float32 [2, 2048, 5632], P(None, 'fsdp', 'tp')
- down_weight_grad: float32 [5632, 2048], P('tp', 'fsdp')
The draws below stay inside these ranges and needn't reach their ends.
Inputs may be any that keep to these rules, and one draw needn't show every extreme that they name: Each row holds the lengths of a sequence's 6 documents; they sum to 1024 and the longest is exactly 512.
All inputs are finite; a program needn't handle non-finite values.
Results may differ from the reference program's by a relative error of at most 0.023.
The reference program's roundings to bfloat16 on the way count: a program that leaves them out, or rounds other values in their place, can miss the bound.
Values may be sent and summed in bfloat16 or wider, within the bound.
No kernel may reach another device: no remote copies, remote signals or barrier semaphores. Data moves between devices by JAX's collectives and lax.ppermute only.
A program may use at most 320 MiB of HBM per device.

```python
import math
import jax
import jax.numpy as jnp
import numpy as np
from jax import lax

D = 2048
HEADS = 32
HD = 64
FF = 5632
ROT = 16
DOCS = 6
SEQS = 4
LEN = 1024
DOC_MOST = 512


def draw_qkv_bias(key, part):
    first_key = jax.random.fold_in(key, 0)
    drawn = jnp.clip(0.5 * jax.random.normal(first_key, (3, HEADS, HD), jnp.float32), -3.0, 3.0)
    return drawn.astype(jnp.bfloat16)


def level_of(key, extent, cuts, low, top_value):
    level = 1.0
    for position, parts in cuts:
        steps = jax.random.uniform(jax.random.fold_in(jax.random.fold_in(key, 6), position), (parts,), jnp.float32, low / len(cuts), top_value / len(cuts))
        level = level * jnp.repeat(jnp.exp(steps), extent[position] // parts).reshape((-1,) + (1,) * (len(extent) - 1 - position))
    return level


def profile(amount, total, limit, skew):
    loads = [(1 << 20) // math.isqrt(standing ** skew) + 1 for standing in range(2, amount + 1)]
    surplus, holding = total - limit - (amount - 1), [1] * (amount - 1)
    while surplus > 0:
        free = [i for i in range(amount - 1) if holding[i] < limit]
        whole, budget = sum([loads[i] for i in free]), surplus
        for i in free:
            extra = min(limit - holding[i], max(1, budget * loads[i] // whole), surplus)
            holding[i] = holding[i] + extra
            surplus = surplus - extra
    return np.array([limit] + holding)


def uneven_parts(key, count, total, limit, slope):
    if count == 2:
        one = jax.random.randint(key, (), max(1, total - limit), min(limit, total - 1) + 1)
        return jnp.stack([one, total - one])
    tallies = jnp.asarray(profile(count, total, limit, slope), jnp.int32)
    couples = (count - 1) // 2
    source_of, taker = tallies[1:1 + 2 * couples:2], tallies[2:2 + 2 * couples:2]
    slack = jnp.minimum(source_of - 1, limit - taker)
    moved = jax.random.randint(jax.random.fold_in(key, 1), (couples,), 0, 1 << 20) % (slack + 1)
    tallies = tallies.at[1:1 + 2 * couples:2].set(source_of - moved).at[2:2 + 2 * couples:2].set(taker + moved)
    return tallies[jax.random.permutation(jax.random.fold_in(key, 2), count)]


def bell_draw(own_key, shape, spread, limit, cuts=(), held_as=jnp.bfloat16):
    array = spread * jax.random.normal(own_key, shape, jnp.float32)
    if cuts:
        array = array * level_of(own_key, shape, cuts, -0.22, 0.18)
    return jnp.clip(array, -limit, limit).astype(held_as)


def setup_inputs(seed: int = 0) -> dict:
    splits = jax.random.split(jax.random.key(seed), 11)
    return {
        "block_input": bell_draw(splits[0], (SEQS, LEN, D), 1.0, 6.0, ((0, 4), (1, 4))),
        "lengths": jax.vmap(lambda own: uneven_parts(own, DOCS, LEN, DOC_MOST, 2))(jax.random.split(splits[1], SEQS)).reshape((SEQS, DOCS)).astype(jnp.int32),
        "norm_scales": jnp.clip(1.0 + 0.18 * jax.random.normal(splits[2], (2, D), jnp.float32), 0.099609375, 1.8984375).astype(jnp.bfloat16),
        "norm_biases": bell_draw(splits[3], (2, D), 0.5, 3.0, ((1, 4),)),
        "qkv_weight": bell_draw(splits[4], (3, D, HEADS * HD), D ** -0.5, 0.125, ((1, 4), (2, 2))),
        "qkv_bias": draw_qkv_bias(jax.random.fold_in(splits[10], 71), 0),
        "out_weight": bell_draw(splits[6], (HEADS * HD, D), (max(1, HEADS * HD // 256)) ** -0.5, 2.0, ((0, 2), (1, 4))),
        "gate_up_weight": bell_draw(splits[7], (2, D, FF), D ** -0.5, 0.125, ((1, 4), (2, 2))),
        "down_weight": bell_draw(splits[8], (FF, D), (FF // 2) ** -0.5, 0.109375, ((0, 2), (1, 4))),
        "out_cotangent": bell_draw(splits[9], (SEQS, LEN, D), 1.0, 6.0, ((0, 4), (1, 4))),
    }


NEG_LARGE = -1e+30
EPS_NORM = 1e-05
ROPE_BASE = 10000.0

def positions_of(doc_lengths, first_token, token_count):
    ends = jnp.cumsum(doc_lengths).astype(jnp.int32)
    starts = ends - doc_lengths.astype(jnp.int32)
    token_index = first_token + jnp.arange(token_count, dtype=jnp.int32)
    doc_begin = lax.optimization_barrier(jnp.max(jnp.where(starts[None, :] <= token_index[:, None], starts[None, :], 0), axis=1)).astype(jnp.int32)
    return (token_index, doc_begin)

def rope_tables(doc_position, rot_dims):
    half_rot = rot_dims // 2
    inverse = ROPE_BASE ** (-(2.0 / rot_dims) * jnp.arange(half_rot, dtype=jnp.float32))
    angles = doc_position.astype(jnp.float32)[:, None] * inverse[None, :]
    return (jnp.cos(angles), jnp.sin(angles))

def rotate(vectors, cosine_table, sine_table, direction):
    half_rot = cosine_table.shape[-1]
    lower_half = vectors[..., :half_rot]
    upper_half = vectors[..., half_rot:2 * half_rot]
    unrotated = vectors[..., 2 * half_rot:]
    cosine_b = cosine_table[:, None, :]
    sine_b = sine_table[:, None, :] * direction
    return jnp.concatenate([lower_half * cosine_b - upper_half * sine_b, upper_half * cosine_b + lower_half * sine_b, unrotated], axis=-1)

def norm_forward(values_in, gain_row, shift_row):
    row_mean = lax.optimization_barrier(jnp.mean(values_in, axis=-1, keepdims=True))
    centered = values_in - row_mean
    variance = lax.optimization_barrier(jnp.mean(centered * centered, axis=-1, keepdims=True))
    inv_std = lax.rsqrt(variance + EPS_NORM)
    normed = centered * inv_std
    return (normed, inv_std, (normed * gain_row + shift_row).astype(jnp.bfloat16))

def norm_backward(grad_out, normed, inv_std, gain_row):
    grad_normed = grad_out * gain_row
    grad_in = inv_std * (grad_normed - lax.optimization_barrier(jnp.mean(grad_normed, axis=-1, keepdims=True)) - normed * lax.optimization_barrier(jnp.mean(grad_normed * normed, axis=-1, keepdims=True)))
    return (grad_in, lax.optimization_barrier(jnp.sum(grad_out * normed, axis=0)), lax.optimization_barrier(jnp.sum(grad_out, axis=0)))

def head_forward(head_q, head_k, head_v, allowed):
    scores = jnp.dot(head_q, head_k.T, preferred_element_type=jnp.float32) * HD ** (-0.5)
    scores = jnp.where(allowed, scores, NEG_LARGE)
    row_max = lax.optimization_barrier(jnp.max(scores, axis=1, keepdims=True))
    weights = jnp.where(allowed, jnp.exp(scores - row_max), 0.0)
    row_sum = lax.optimization_barrier(jnp.sum(weights, axis=1, keepdims=True))
    head_out = (jnp.dot(weights.astype(jnp.bfloat16), head_v, preferred_element_type=jnp.float32) / row_sum).astype(jnp.bfloat16)
    return (head_out, (row_max + jnp.log(row_sum))[:, 0])

def head_backward(head_q, head_k, head_v, head_out, head_grad, log_total, allowed):
    scores = jnp.dot(head_q, head_k.T, preferred_element_type=jnp.float32) * HD ** (-0.5)
    scores = jnp.where(allowed, scores, NEG_LARGE)
    weights = jnp.where(allowed, jnp.exp(scores - log_total[:, None]), 0.0)
    grad_weights = jnp.dot(head_grad, head_v.T, preferred_element_type=jnp.float32)
    delta = lax.optimization_barrier(jnp.sum(head_grad.astype(jnp.float32) * head_out.astype(jnp.float32), axis=1, keepdims=True))
    grad_scores = weights * (grad_weights - delta)
    weights_b = weights.astype(jnp.bfloat16)
    grad_scores_b = grad_scores.astype(jnp.bfloat16)
    grad_v = jnp.dot(weights_b.T, head_grad, preferred_element_type=jnp.float32)
    grad_k = jnp.dot(grad_scores_b.T, head_q, preferred_element_type=jnp.float32) * HD ** (-0.5)
    grad_q = jnp.dot(grad_scores_b, head_k, preferred_element_type=jnp.float32) * HD ** (-0.5)
    return (grad_q, grad_k, grad_v)

def reference(block_input, lengths, norm_scales, norm_biases, qkv_weight, qkv_bias, out_weight, gate_up_weight, down_weight, out_cotangent):
    gains = norm_scales.astype(jnp.float32)
    shifts = norm_biases.astype(jnp.float32)
    qkv_full = qkv_weight.astype(jnp.float32)
    head_cols = HEADS * HD
    bias_full = qkv_bias.astype(jnp.float32).reshape(3, 1, head_cols)
    gate_up_full = gate_up_weight.astype(jnp.float32)

    def heads_first(matrix):
        return jnp.transpose(matrix.reshape(LEN, HEADS, HD), (1, 0, 2))

    def tokens_first(stacked):
        return jnp.transpose(stacked, (1, 0, 2))

    def one_sequence(totals, inputs):
        seq_input, doc_lengths, seq_cot = inputs
        token_index, doc_begin = positions_of(doc_lengths, jnp.int32(0), LEN)
        allowed = (token_index[None, :] <= token_index[:, None]) & (token_index[None, :] >= doc_begin[:, None])
        cosine_table, sine_table = rope_tables(token_index - doc_begin, ROT)
        residual_in = seq_input.astype(jnp.float32)
        normed_one, inv_std_one, ln_one = norm_forward(residual_in, gains[0], shifts[0])
        projected = jnp.einsum('nd,cdf->cnf', ln_one.astype(jnp.float32), qkv_full) + bias_full
        queries = rotate(projected[0].reshape(LEN, HEADS, HD), cosine_table, sine_table, 1.0).astype(jnp.bfloat16)
        keys_all = rotate(projected[1].reshape(LEN, HEADS, HD), cosine_table, sine_table, 1.0).astype(jnp.bfloat16)
        values_all = projected[2].reshape(LEN, HEADS, HD).astype(jnp.bfloat16)
        head_queries = tokens_first(queries)
        head_keys = tokens_first(keys_all)
        head_values = tokens_first(values_all)

        def forward_head(group):
            return head_forward(group[0], group[1], group[2], allowed)
        head_out, log_total = lax.map(forward_head, (head_queries, head_keys, head_values))
        attn_out = tokens_first(head_out).reshape(LEN, head_cols)
        hidden_in = residual_in + jnp.dot(attn_out, out_weight, preferred_element_type=jnp.float32)
        normed_two, inv_std_two, ln_two = norm_forward(hidden_in, gains[1], shifts[1])
        gate_up = jnp.einsum('nd,cdf->cnf', ln_two.astype(jnp.float32), gate_up_full)
        gate_proj = gate_up[0]
        up_proj = gate_up[1]
        gate_sigmoid = jax.nn.sigmoid(gate_proj)
        gate_act = gate_proj * gate_sigmoid
        hidden_units = (gate_act * up_proj).astype(jnp.bfloat16)
        block_out = (hidden_in + jnp.dot(hidden_units, down_weight, preferred_element_type=jnp.float32)).astype(jnp.bfloat16)
        grad_hidden = jnp.dot(seq_cot, down_weight.T, preferred_element_type=jnp.float32)
        grad_down = jnp.dot(hidden_units.T, seq_cot, preferred_element_type=jnp.float32)
        grad_gate_up = jnp.stack([grad_hidden * up_proj * gate_sigmoid * (1.0 + gate_proj * (1.0 - gate_sigmoid)), grad_hidden * gate_act]).astype(jnp.bfloat16)
        grad_gate_up_w = jnp.einsum('nd,cnf->cdf', ln_two.astype(jnp.float32), grad_gate_up.astype(jnp.float32))
        grad_ln_two = jnp.einsum('cnf,cdf->nd', grad_gate_up.astype(jnp.float32), gate_up_full)
        grad_from_two, scale_two, shift_two = norm_backward(grad_ln_two, normed_two, inv_std_two, gains[1])
        grad_hidden_in = seq_cot.astype(jnp.float32) + grad_from_two
        grad_residual = grad_hidden_in.astype(jnp.bfloat16)
        grad_out_w = jnp.dot(attn_out.T, grad_residual, preferred_element_type=jnp.float32)
        grad_attn_out = jnp.dot(grad_residual, out_weight.T, preferred_element_type=jnp.float32).astype(jnp.bfloat16)
        head_grad_out = heads_first(grad_attn_out)

        def backward_head(group):
            return head_backward(group[0], group[1], group[2], group[3], group[4], group[5], allowed)
        grad_q, grad_k, grad_v = lax.map(backward_head, (head_queries, head_keys, head_values, head_out, head_grad_out, log_total))
        grad_q = rotate(tokens_first(grad_q), cosine_table, sine_table, -1.0).reshape(LEN, head_cols)
        grad_k = rotate(tokens_first(grad_k), cosine_table, sine_table, -1.0).reshape(LEN, head_cols)
        grad_v = tokens_first(grad_v).reshape(LEN, head_cols)
        grad_proj = jnp.stack([grad_q, grad_k, grad_v])
        grad_bias = lax.optimization_barrier(jnp.sum(grad_proj, axis=1)).reshape(3, HEADS, HD)
        grad_proj_b = grad_proj.astype(jnp.bfloat16)
        grad_qkv_w = jnp.einsum('nd,cnf->cdf', ln_one.astype(jnp.float32), grad_proj_b.astype(jnp.float32))
        grad_ln_one = jnp.einsum('cnf,cdf->nd', grad_proj_b.astype(jnp.float32), qkv_full)
        grad_from_one, scale_one, shift_one = norm_backward(grad_ln_one, normed_one, inv_std_one, gains[0])
        input_grad = grad_hidden_in + grad_from_one
        terms = (jnp.stack([scale_one, scale_two]), jnp.stack([shift_one, shift_two]), grad_qkv_w, grad_bias, grad_out_w, grad_gate_up_w, grad_down)
        totals = jax.tree.map(lambda left, right: left + right, totals, terms)
        return (totals, (block_out, input_grad))
    start_totals = (jnp.zeros((2, D), jnp.float32), jnp.zeros((2, D), jnp.float32), jnp.zeros((3, D, head_cols), jnp.float32), jnp.zeros((3, HEADS, HD), jnp.float32), jnp.zeros((head_cols, D), jnp.float32), jnp.zeros((2, D, FF), jnp.float32), jnp.zeros((FF, D), jnp.float32))
    totals, outputs = lax.scan(one_sequence, start_totals, (block_input, lengths, out_cotangent))
    return (outputs[0], outputs[1], totals[0], totals[1], totals[2], totals[3], totals[4], totals[5], totals[6])
```

```python
import functools

import jax
import jax.numpy as jnp
from jax import lax
from jax.experimental import pallas as pl
from jax.experimental.pallas import tpu as pltpu
from jax.sharding import Mesh
from jax.sharding import PartitionSpec as P

HD = 64
ROT = 16
DOC_MOST = 512
LANES = 128

NEG_LARGE = -1e30
EPS_NORM = 1e-05
ROPE_BASE = 10000.0
F32 = jnp.float32
BF16 = jnp.bfloat16


def pick(array, index, axis=0):
    return lax.dynamic_index_in_dim(array, index, axis, keepdims=False)


def swap(array, axis_name):
    return lax.ppermute(array, axis_name, [(0, 1), (1, 0)])


def after(array, *earlier):
    return lax.optimization_barrier((array, *earlier))[0]


def ordered(first_here, mine, theirs, axis=0):
    lower = jnp.where(first_here, mine, theirs)
    upper = jnp.where(first_here, theirs, mine)
    return jnp.stack([lower, upper], axis=axis)


def norm_stats(values_in):
    row_mean = jnp.mean(values_in, axis=-1, keepdims=True)
    centered = values_in - row_mean
    variance = jnp.mean(centered * centered, axis=-1, keepdims=True)
    inv_std = lax.rsqrt(variance + EPS_NORM)
    return centered * inv_std, inv_std


def norm_backward(grad_out, normed, inv_std, gain_row):
    grad_normed = grad_out * gain_row
    grad_in = inv_std * (
        grad_normed
        - jnp.mean(grad_normed, axis=-1, keepdims=True)
        - normed * jnp.mean(grad_normed * normed, axis=-1, keepdims=True)
    )
    return (grad_in, jnp.sum(grad_out * normed, axis=0), jnp.sum(grad_out, axis=0))


def turn(values, cosine, sine_up, sine_down, direction):
    lanes = values.shape[-1]
    from_above = pltpu.roll(values, lanes - ROT // 2, 1)
    from_below = pltpu.roll(values, ROT // 2, 1)
    return values * cosine + direction * (from_above * sine_up + from_below * sine_down)


def dot_nt(left, right):
    return lax.dot_general(left, right, (((1,), (1,)), ((), ())), preferred_element_type=F32)


def dot_tn(left, right):
    return lax.dot_general(left, right, (((0,), (0,)), ((), ())), preferred_element_type=F32)


def dot_nn(left, right):
    return jnp.dot(left, right, preferred_element_type=F32)


def project_kernel(x_ref, w_ref, b_ref, cos_ref, up_ref, down_ref, o_ref):
    total = dot_nn(x_ref[...], w_ref[0]) + b_ref[0]
    which = pl.program_id(0)

    @pl.when(which < 2)
    def _():
        for at in range(0, total.shape[1], LANES):
            o_ref[0, :, at : at + LANES] = turn(
                total[:, at : at + LANES], cos_ref[...], up_ref[...], down_ref[...], 1.0
            ).astype(BF16)

    @pl.when(which == 2)
    def _():
        o_ref[0] = total.astype(BF16)


def project(normed, weight, bias, tables):
    rows, depth = normed.shape
    cols = weight.shape[2]
    tile = min(cols, 2 * LANES)
    table_spec = pl.BlockSpec((rows, LANES), lambda c, j: (0, 0))
    return pl.pallas_call(
        project_kernel,
        grid=(3, cols // tile),
        in_specs=[
            pl.BlockSpec((rows, depth), lambda c, j: (0, 0)),
            pl.BlockSpec((1, depth, tile), lambda c, j: (c, 0, j)),
            pl.BlockSpec((1, 1, tile), lambda c, j: (c, 0, j)),
            table_spec,
            table_spec,
            table_spec,
        ],
        out_specs=pl.BlockSpec((1, rows, tile), lambda c, j: (c, 0, j)),
        out_shape=jax.ShapeDtypeStruct((3, rows, cols), BF16),
        compiler_params=pltpu.CompilerParams(vmem_limit_bytes=40 << 20),
        name="project",
    )(normed, weight, bias, *tables)


def visible_of(chunk, begin, key_chunk, rows):
    query = chunk * rows + lax.broadcasted_iota(jnp.int32, (rows, rows), 0)
    key = key_chunk * rows + lax.broadcasted_iota(jnp.int32, (rows, rows), 1)
    return (key <= query) & (key >= begin)


def attend_kernel(parts, chunk_ref, q_ref, begin_ref, *refs):
    kv_refs, (o_ref, l_ref) = refs[:parts], refs[parts:]
    rows = q_ref.shape[1]
    query = q_ref[0]
    chunk = chunk_ref[0]
    first = lax.broadcasted_iota(jnp.int32, query.shape, 1) < HD
    seen = [visible_of(chunk, begin_ref[...], chunk - b, rows) for b in range(parts)]
    outs, logs = [], []
    for head in range(2):
        own = jnp.where(first if head == 0 else ~first, query, jnp.zeros_like(query))
        scores = [
            jnp.where(seen[b], dot_nt(own, kv_refs[b][0]) * (HD**-0.5), NEG_LARGE)
            for b in range(parts)
        ]
        top = functools.reduce(
            jnp.maximum, [jnp.max(s, axis=1, keepdims=True) for s in scores]
        )
        weights = [jnp.exp(s - top) for s in scores]
        total = sum(jnp.sum(w, axis=1, keepdims=True) for w in weights)
        mixed = sum(dot_nn(w.astype(BF16), kv_refs[b][1]) for b, w in enumerate(weights))
        outs.append(mixed / total)
        logs.append(top + jnp.log(total))
    o_ref[...] = jnp.where(first, outs[0], outs[1]).astype(BF16)
    l_ref[...] = jnp.where(first, logs[0], logs[1])


def attend(chunk, queries, begin, kvs):
    _, tokens, cols = queries.shape
    rows = tokens // 2
    kv_spec = pl.BlockSpec((2, rows, LANES), lambda s, j, *_: (0, s, j))
    flat_spec = pl.BlockSpec((rows, LANES), lambda s, j, *_: (s, j))
    return pl.pallas_call(
        functools.partial(attend_kernel, len(kvs)),
        grid_spec=pltpu.PrefetchScalarGridSpec(
            num_scalar_prefetch=1,
            grid=(2, cols // LANES),
            in_specs=[
                pl.BlockSpec((1, rows, LANES), lambda s, j, *_: (0, s, j)),
                pl.BlockSpec((rows, 1), lambda s, j, *_: (s, 0)),
            ]
            + [kv_spec] * len(kvs),
            out_specs=[flat_spec, flat_spec],
        ),
        out_shape=[
            jax.ShapeDtypeStruct((tokens, cols), BF16),
            jax.ShapeDtypeStruct((tokens, cols), F32),
        ],
        compiler_params=pltpu.CompilerParams(vmem_limit_bytes=40 << 20),
        name="attend",
    )(chunk, queries, begin, *kvs)


def attend_back_kernel(parts, chunk_ref, q_ref, begin_ref, do_ref, o_ref, l_ref, *refs):
    cos_ref, up_ref, down_ref = refs[:3]
    kv_refs = refs[3 : 3 + parts]
    gq_ref, bias_ref = refs[3 + parts : 5 + parts]
    gkv_refs = refs[5 + parts :]
    rows = q_ref.shape[1]
    query = q_ref[0]
    grad_out = do_ref[...]
    chunk = chunk_ref[0]
    first = lax.broadcasted_iota(jnp.int32, query.shape, 1) < HD
    product = grad_out.astype(F32) * o_ref[...].astype(F32)
    grad_q = []
    grad_k = [0.0] * parts
    grad_v = [0.0] * parts
    for head in range(2):
        here = first if head == 0 else ~first
        own = jnp.where(here, query, jnp.zeros_like(query))
        own_grad = jnp.where(here, grad_out, jnp.zeros_like(grad_out))
        delta = jnp.sum(jnp.where(here, product, 0.0), axis=1, keepdims=True)
        log_total = l_ref[:, head * HD : head * HD + 1]
        into_q = 0.0
        for b in range(parts):
            seen = visible_of(chunk, begin_ref[...], chunk - b, rows)
            scores = dot_nt(own, kv_refs[b][0]) * (HD**-0.5)
            weights = jnp.exp(jnp.where(seen, scores, NEG_LARGE) - log_total)
            grad_w = dot_nt(own_grad, kv_refs[b][1])
            grad_s = (weights * (grad_w - delta)).astype(BF16)
            grad_v[b] += dot_tn(weights.astype(BF16), own_grad)
            grad_k[b] += dot_tn(grad_s, own)
            into_q += dot_nn(grad_s, kv_refs[b][0])
        grad_q.append(into_q)
    scale = HD**-0.5
    turned = turn(
        jnp.where(first, grad_q[0], grad_q[1]) * scale,
        cos_ref[...],
        up_ref[...],
        down_ref[...],
        -1.0,
    )
    gq_ref[...] = turned.astype(BF16)
    bias_ref[0] = jnp.sum(turned, axis=0, keepdims=True)
    for b in range(parts):
        gkv_refs[b][0] = (grad_k[b] * scale).astype(gkv_refs[b].dtype)
        gkv_refs[b][1] = grad_v[b].astype(gkv_refs[b].dtype)


def attend_back(chunk, queries, begin, grad_out, attn_out, log_total, tables, kvs):
    _, tokens, cols = queries.shape
    rows = tokens // 2
    kv_spec = pl.BlockSpec((2, rows, LANES), lambda s, j, *_: (0, s, j))
    flat_spec = pl.BlockSpec((rows, LANES), lambda s, j, *_: (s, j))
    table_spec = pl.BlockSpec((rows, LANES), lambda s, j, *_: (s, 0))
    return pl.pallas_call(
        functools.partial(attend_back_kernel, len(kvs)),
        grid_spec=pltpu.PrefetchScalarGridSpec(
            num_scalar_prefetch=1,
            grid=(2, cols // LANES),
            in_specs=[
                pl.BlockSpec((1, rows, LANES), lambda s, j, *_: (0, s, j)),
                pl.BlockSpec((rows, 1), lambda s, j, *_: (s, 0)),
                flat_spec,
                flat_spec,
                flat_spec,
                table_spec,
                table_spec,
                table_spec,
            ]
            + [kv_spec] * len(kvs),
            out_specs=[flat_spec, pl.BlockSpec((1, 1, LANES), lambda s, j, *_: (s, 0, j))]
            + [kv_spec] * len(kvs),
        ),
        out_shape=[
            jax.ShapeDtypeStruct((tokens, cols), BF16),
            jax.ShapeDtypeStruct((2, 1, cols), F32),
        ]
        + [
            jax.ShapeDtypeStruct((2, tokens, cols), F32 if b == 0 else BF16)
            for b in range(len(kvs))
        ],
        compiler_params=pltpu.CompilerParams(vmem_limit_bytes=40 << 20),
        name="attend_back",
    )(chunk, queries, begin, grad_out, attn_out, log_total, *tables, *kvs)


def finish_kernel(here_ref, came_ref, cos_ref, up_ref, down_ref, g_ref, bias_ref):
    grad_k = here_ref[0] + came_ref[0].astype(F32)
    grad_v = here_ref[1] + came_ref[1].astype(F32)
    for at in range(0, grad_k.shape[1], LANES):
        turned = turn(
            grad_k[:, at : at + LANES], cos_ref[...], up_ref[...], down_ref[...], -1.0
        )
        g_ref[0, :, at : at + LANES] = turned.astype(BF16)
        bias_ref[0, :, at : at + LANES] = jnp.sum(turned, axis=0, keepdims=True)
    g_ref[1] = grad_v.astype(BF16)
    bias_ref[1] = jnp.sum(grad_v, axis=0, keepdims=True)


def finish_keys(here, came, tables):
    return pl.pallas_call(
        finish_kernel,
        out_shape=[
            jax.ShapeDtypeStruct(here.shape, BF16),
            jax.ShapeDtypeStruct((2, 1, here.shape[2]), F32),
        ],
        compiler_params=pltpu.CompilerParams(vmem_limit_bytes=40 << 20),
        name="finish_keys",
    )(here, came, *tables)


def fetch_block(weight, split_axis, join_axis, fx, core, gate=None):
    half = weight.shape[split_axis] // 2
    mine = lax.dynamic_slice_in_dim(weight, fx * half, half, split_axis)
    other = lax.dynamic_slice_in_dim(weight, (1 - fx) * half, half, split_axis)
    if gate is not None:
        other = after(other, gate)
    across = swap(other, "fx")
    beside = swap(mine, "core")
    corner = swap(across, "core")
    width = mine.shape[join_axis]
    shape = list(mine.shape)
    shape[join_axis] = 4 * width
    whole = jnp.zeros(shape, weight.dtype)
    for piece, chip, part in (
        (mine, fx, core),
        (beside, fx, 1 - core),
        (across, 1 - fx, core),
        (corner, 1 - fx, 1 - core),
    ):
        whole = lax.dynamic_update_slice_in_dim(
            whole, piece, (chip * 2 + part) * width, join_axis
        )
    return whole, across


def scatter_plane(partial, fx, tp, sizes):
    n_fx, n_tp = sizes
    rows = partial.shape[0] // (n_fx * n_tp)
    wide = partial.shape[1]
    blocks = partial.reshape(n_fx, n_tp, rows, wide)
    if n_fx != 2 or n_tp != 2:
        return lax.psum_scatter(
            blocks.reshape(n_fx * n_tp, rows, wide), ("fx", "tp"), scatter_dimension=0
        ).astype(F32)
    half = wide // 2
    left, right = blocks[..., :half], blocks[..., half:]
    a_in = swap(pick(left, 1 - fx), "fx")
    b_in = swap(pick(right, 1 - tp, 1), "tp")
    a_sum = pick(left, fx).astype(F32) + a_in.astype(F32)
    b_sum = pick(right, tp, 1).astype(F32) + b_in.astype(F32)
    a_last = swap(pick(a_sum, 1 - tp).astype(BF16), "tp")
    b_last = swap(pick(b_sum, 1 - fx).astype(BF16), "fx")
    return jnp.concatenate(
        [pick(a_sum, tp) + a_last.astype(F32), pick(b_sum, fx) + b_last.astype(F32)], axis=1
    )


def gather_plane(share, fx, tp, sizes):
    n_fx, n_tp = sizes
    rows, wide = share.shape
    if n_fx != 2 or n_tp != 2:
        return lax.all_gather(share, ("fx", "tp"), axis=0, tiled=True)
    half = wide // 2
    left, right = share[:, :half], share[:, half:]
    a_pair = ordered(tp == 0, left, swap(left, "tp"))
    b_pair = ordered(fx == 0, right, swap(right, "fx"))
    a_all = ordered(fx == 0, a_pair, swap(a_pair, "fx"))
    b_all = ordered(tp == 0, b_pair, swap(b_pair, "tp"), axis=1)
    return jnp.concatenate([a_all, b_all], axis=-1).reshape(4 * rows, wide)


def gather_tp(share, tp, n_tp):
    if n_tp != 2:
        return lax.all_gather(share, "tp", axis=0, tiled=True)
    return ordered(tp == 0, share, swap(share, "tp")).reshape(2 * share.shape[0], -1)


def line_scatter(segment, ctx, count):
    right = left = None
    for step in range(1, count):
        going = segment(jnp.clip(count - step + ctx, 0, count - 1))
        coming = segment(jnp.clip(ctx - count + step, 0, count - 1))
        if right is not None:
            going = (going.astype(F32) + right.astype(F32)).astype(BF16)
            coming = (coming.astype(F32) + left.astype(F32)).astype(BF16)
        right = lax.ppermute(
            going, "ctx", [(i, i + 1) for i in range(count - 1) if step >= i + 1]
        )
        left = lax.ppermute(
            coming, "ctx", [(i, i - 1) for i in range(1, count) if step >= count - i]
        )
    total = segment(ctx).astype(F32) + right.astype(F32) + left.astype(F32)
    return total.astype(BF16)


def line_gather(piece, ctx, count):
    rights, lefts = [], []
    going = coming = piece
    for step in range(1, count):
        going = lax.ppermute(going, "ctx", [(i, i + 1) for i in range(step - 1, count - 1)])
        coming = lax.ppermute(coming, "ctx", [(i, i - 1) for i in range(1, count - step + 1)])
        rights.append(going)
        lefts.append(coming)
    found = [(ctx, piece)]
    for step in range(1, count):
        found.append(
            (
                lax.rem(ctx - step + count, count),
                jnp.where(ctx >= step, rights[step - 1], lefts[count - 1 - step]),
            )
        )
    return found


def weight_sum_columns(grad, fx, ctx, count):
    kinds, _, rows, cols = grad.shape
    part = rows // count
    split = grad.reshape(kinds, 2, count, part, cols)
    mine = line_scatter(lambda i: pick(split, i, 2), ctx, count)
    keep, give = pick(mine, fx, 1), pick(mine, 1 - fx, 1)
    pair = ordered(fx == 0, keep, swap(give, "fx"))
    out = jnp.zeros((kinds, rows, 2 * cols), F32)
    for where, piece in line_gather(pair, ctx, count):
        for chip in range(2):
            out = lax.dynamic_update_slice(
                out, piece[chip].astype(F32), (0, where * part, chip * cols)
            )
    return out


def weight_sum_rows(grad, fx, ctx, count):
    rows = grad.shape[0]
    cols = grad.shape[1] // 2
    part = rows // count
    split = grad.reshape(count, part, 2 * cols)
    mine = line_scatter(lambda i: pick(split, i, 0), ctx, count)
    keep = lax.dynamic_slice_in_dim(mine, fx * cols, cols, 1)
    give = lax.dynamic_slice_in_dim(mine, (1 - fx) * cols, cols, 1)
    pair = ordered(fx == 0, keep, swap(give, "fx"))
    out = jnp.zeros((2, rows, cols), F32)
    for where, piece in line_gather(pair, ctx, count):
        out = lax.dynamic_update_slice(out, piece.astype(F32), (0, where * part, 0))
    return out.reshape(2 * rows, cols)


def shards(
    sizes,
    block_input,
    lengths,
    norm_scales,
    norm_biases,
    qkv_weight,
    qkv_bias,
    out_weight,
    gate_up_weight,
    down_weight,
    out_cotangent,
):
    n_fx, n_ctx, n_tp = sizes
    plane = (n_fx, n_tp)
    fx, core = lax.axis_index("fx"), lax.axis_index("core")
    ctx, tp = lax.axis_index("ctx"), lax.axis_index("tp")
    fsdp = fx * 2 + core
    rows, width = block_input.shape[1:]
    block = width // (n_fx * 2)
    share_rows = rows // n_tp
    share_at = tp * share_rows
    tp_heads = qkv_bias.shape[1]
    heads = tp_heads // 2
    cols = heads * HD

    input_far = swap(block_input[0], "fx")
    w_qkv, qkv_far = fetch_block(qkv_weight, 2, 1, fx, core)
    w_out, out_far = fetch_block(out_weight, 0, 1, fx, core, qkv_far)
    w_gate_up, gate_far = fetch_block(gate_up_weight, 2, 1, fx, core, qkv_far)
    small = jnp.concatenate(
        [norm_scales.reshape(-1), norm_biases.reshape(-1), qkv_bias.reshape(-1)]
    )
    small = lax.all_gather(small, ("fx", "core"), axis=0).astype(F32)
    gains = small[:, : 2 * block].reshape(-1, 2, block).swapaxes(0, 1).reshape(2, width)
    shifts = (
        small[:, 2 * block : 4 * block].reshape(-1, 2, block).swapaxes(0, 1).reshape(2, width)
    )
    bias = small[:, 4 * block :].reshape(-1, 3, tp_heads, qkv_bias.shape[2])
    bias = bias.transpose(1, 2, 0, 3).reshape(3, tp_heads * HD)
    bias = lax.dynamic_slice_in_dim(bias, fx * cols, cols, 1).reshape(3, 1, cols)

    both_lengths = ordered(fx == 0, lengths[0], swap(lengths[0], "fx"))
    starts = jnp.cumsum(both_lengths, axis=1) - both_lengths
    token = ctx * rows + jnp.arange(rows, dtype=jnp.int32)
    begin = jnp.max(
        jnp.where(starts[:, None, :] <= token[None, :, None], starts[:, None, :], 0), axis=2
    )
    position = (token[None, :] - begin).reshape(-1)
    begin = begin.reshape(-1, 1)
    lane = jnp.arange(LANES, dtype=jnp.int32) % HD
    inverse = ROPE_BASE ** (-(2.0 / ROT) * (lane % (ROT // 2)).astype(F32))
    angle = position.astype(F32)[:, None] * inverse[None, :]
    sine = jnp.sin(angle)
    tables = (
        jnp.where(lane < ROT, jnp.cos(angle), 1.0),
        jnp.where(lane < ROT // 2, -sine, 0.0),
        jnp.where((lane >= ROT // 2) & (lane < ROT), sine, 0.0),
    )
    chunk = ctx.astype(jnp.int32).reshape(1)

    tokens_in = ordered(fx == 0, block_input[0], input_far).reshape(2 * rows, width).astype(F32)
    ln_one = (norm_stats(tokens_in)[0] * gains[0] + shifts[0]).astype(BF16)
    qkv = project(ln_one, w_qkv, bias, tables)
    earlier = min(n_ctx - 1, -(-(DOC_MOST - 1) // rows))
    kvs = [qkv[1:]]
    for step in range(earlier):
        kvs.append(
            lax.ppermute(kvs[-1], "ctx", [(i, i + 1) for i in range(step, n_ctx - 1)])
        )
    cot_far = swap(after(out_cotangent[0], out_far), "fx")
    cot = ordered(fx == 0, out_cotangent[0], cot_far).reshape(2 * rows, width)
    w_down, _ = fetch_block(down_weight, 0, 1, fx, core, gate_far)
    attn_out, log_total = attend(chunk, qkv, begin, kvs)
    attn_share = scatter_plane(dot_nn(attn_out, w_out).astype(BF16), fx, tp, plane)
    input_share = lax.dynamic_slice_in_dim(block_input[0], share_at, share_rows, 0).astype(F32)
    hidden_share = input_share + attn_share
    normed_two, inv_std_two = norm_stats(hidden_share)
    ln_two = gather_plane((normed_two * gains[1] + shifts[1]).astype(BF16), fx, tp, plane)

    gate_up = jnp.einsum("nd,cdf->cnf", ln_two, w_gate_up, preferred_element_type=F32)
    grad_hidden = dot_nt(cot, w_down)
    gate, up = gate_up[0], gate_up[1]
    gate_sigmoid = jax.nn.sigmoid(gate)
    gate_act = gate * gate_sigmoid
    hidden_units = (gate_act * up).astype(BF16)
    grad_gate_up = jnp.stack(
        [
            grad_hidden * up * gate_sigmoid * (1.0 + gate * (1.0 - gate_sigmoid)),
            grad_hidden * gate_act,
        ]
    ).astype(BF16)
    grad_ln_two_share = scatter_plane(
        jnp.einsum("cnf,cdf->nd", grad_gate_up, w_gate_up, preferred_element_type=F32).astype(
            BF16
        ),
        fx,
        tp,
        plane,
    )
    ffn_share = scatter_plane(dot_nn(hidden_units, w_down).astype(BF16), fx, tp, plane)
    block_out = gather_tp((hidden_share + ffn_share).astype(BF16), tp, n_tp)

    def own_columns(array):
        split = array.reshape(array.shape[0], n_fx, 2, block)
        keep, give = pick(split, core, 2), pick(split, 1 - core, 2)
        return jnp.concatenate([keep, swap(give, "core")], axis=0).reshape(-1, n_fx * block)

    def both_cores(array, axis=0):
        return jnp.concatenate([array, swap(array, "core")], axis=axis)

    grad_down = dot_tn(both_cores(hidden_units), own_columns(cot)).astype(BF16)
    down_grad = weight_sum_rows(grad_down, fx, ctx, n_ctx)
    grad_gate_up_w = jnp.einsum(
        "nd,cnf->cdf",
        own_columns(ln_two),
        both_cores(grad_gate_up, 1),
        preferred_element_type=F32,
    ).astype(BF16)
    gate_up_grad = weight_sum_columns(
        grad_gate_up_w.reshape(2, n_fx, block, -1), fx, ctx, n_ctx
    )

    grad_from_two, scale_two, shift_two = norm_backward(
        grad_ln_two_share, normed_two, inv_std_two, gains[1]
    )
    cot_share = lax.dynamic_slice_in_dim(out_cotangent[0], share_at, share_rows, 0)
    grad_hidden_share = cot_share.astype(F32) + grad_from_two
    grad_residual = gather_plane(grad_hidden_share.astype(BF16), fx, tp, plane)

    grad_attn = dot_nt(grad_residual, w_out).astype(BF16)
    grad_out_w = dot_tn(both_cores(attn_out), own_columns(grad_residual)).astype(BF16)
    out_grad = weight_sum_rows(grad_out_w, fx, ctx, n_ctx)
    grad_q, bias_q, *grad_kvs = attend_back(
        chunk, qkv, begin, grad_attn, attn_out, log_total, tables, kvs
    )
    came = None
    for step in range(earlier, 0, -1):
        going = grad_kvs[step]
        if came is not None:
            going = (going.astype(F32) + came.astype(F32)).astype(BF16)
        came = lax.ppermute(going, "ctx", [(i, i - 1) for i in range(step, n_ctx)])
    grad_kv, bias_kv = finish_keys(grad_kvs[0], came, tables)
    grad_proj = jnp.concatenate([grad_q[None], grad_kv], axis=0)
    bias_part = jnp.concatenate([jnp.sum(bias_q, axis=0)[None], bias_kv], axis=0)
    grad_ln_one_share = scatter_plane(
        jnp.einsum("cnm,cdm->nd", grad_proj, w_qkv, preferred_element_type=F32).astype(BF16),
        fx,
        tp,
        plane,
    )
    grad_qkv_w = jnp.einsum(
        "nd,cnm->cdm",
        own_columns(ln_one),
        both_cores(grad_proj, 1),
        preferred_element_type=F32,
    ).astype(BF16)
    qkv_grad = weight_sum_columns(grad_qkv_w.reshape(3, n_fx, block, cols), fx, ctx, n_ctx)
    normed_one, inv_std_one = norm_stats(input_share)
    grad_from_one, scale_one, shift_one = norm_backward(
        grad_ln_one_share, normed_one, inv_std_one, gains[0]
    )
    input_grad = gather_tp((grad_hidden_share + grad_from_one).astype(BF16), tp, n_tp)

    norm_part = jnp.stack([scale_one, scale_two, shift_one, shift_two])
    slots = jnp.zeros((n_tp, n_fx, 3, cols), F32)
    slots = lax.dynamic_update_slice(slots, bias_part.reshape(1, 1, 3, cols), (tp, fx, 0, 0))
    summed = lax.psum(
        jnp.concatenate([norm_part.reshape(-1), slots.reshape(-1)]),
        ("fx", "core", "ctx", "tp"),
    )
    norm_total = lax.dynamic_slice_in_dim(
        summed[: 4 * width].reshape(4, width), fsdp * block, block, 1
    )
    bias_total = pick(summed[4 * width :].reshape(n_tp, n_fx, 3, heads, HD), tp)
    bias_total = bias_total.swapaxes(0, 1).reshape(3, tp_heads, HD)
    part = HD // (n_fx * 2)
    bias_total = lax.dynamic_slice_in_dim(bias_total, fsdp * part, part, 2)
    return (
        block_out[None],
        input_grad.astype(F32)[None],
        norm_total[0:2],
        norm_total[2:4],
        qkv_grad,
        bias_total,
        out_grad,
        gate_up_grad,
        down_grad,
    )


def solution(mesh):
    n_fsdp, n_ctx, n_tp = (mesh.shape[name] for name in ("fsdp", "ctx", "tp"))
    inner = Mesh(
        mesh.devices.reshape(n_fsdp // 2, 2, n_ctx, n_tp), ("fx", "core", "ctx", "tp")
    )
    fsdp = ("fx", "core")
    in_specs = (
        P(fsdp, "ctx", None),
        P(fsdp, None),
        P(None, fsdp),
        P(None, fsdp),
        P(None, fsdp, "tp"),
        P(None, "tp", fsdp),
        P("tp", fsdp),
        P(None, fsdp, "tp"),
        P("tp", fsdp),
        P(fsdp, "ctx", None),
    )
    out_specs = (
        P(fsdp, "ctx", None),
        P(fsdp, "ctx", None),
        P(None, fsdp),
        P(None, fsdp),
        P(None, fsdp, "tp"),
        P(None, "tp", fsdp),
        P("tp", fsdp),
        P(None, fsdp, "tp"),
        P("tp", fsdp),
    )
    return jax.shard_map(
        functools.partial(shards, (n_fsdp // 2, n_ctx, n_tp)),
        mesh=inner,
        in_specs=in_specs,
        out_specs=out_specs,
        check_vma=False,
    )
```
